32 devices in a mesh: dp: 16 (over z, y, core), tensor: 2 (over x).
Axes of the slice: x: 2, y: 2, z: 4, core: 2. Of those that a mesh axis runs over, the one named last changes fastest.
Arguments:
- block_input: bfloat16 [160, 197, 768], P('dp'), may hold values from -6 to 6
- image_counts: int32 [16], P('dp'), may hold values from 1 to 10, 88 in all
- first_norm_gain: float32 [768], replicated, may hold values from 0.1 to 1.9
- first_norm_bias: float32 [768], replicated, may hold values from -3 to 3
- w_qkv: bfloat16 [3, 768, 768], P(None, None, 'tensor'), may hold values from -8 to 8
- qv_bias: float32 [2, 768], P(None, 'tensor'), may hold values from -3 to 3
- w_out: bfloat16 [768, 768], P('tensor'), may hold values from -0.75 to 0.75
- b_out: float32 [768], replicated, may hold values from -3 to 3
- second_norm_gain: float32 [768], replicated, may hold values from 0.1 to 1.9
- second_norm_bias: float32 [768], replicated, may hold values from -3 to 3
- w_fc1: bfloat16 [768, 3072], P(None, 'tensor'), may hold values from -0.21875 to 0.21875
- b_fc1: float32 [3072], P('tensor'), may hold values from -3 to 3
- w_fc2: bfloat16 [3072, 768], P('tensor'), may hold values from -0.109375 to 0.109375
- b_fc2: float32 [768], replicated, may hold values from -3 to 3
- cotangent: bfloat16 [160, 197, 768], P('dp'), may hold values from -6 to 6
Outputs:
- block_out: bfloat16 [160, 197, 768], P('dp')
- gradient_of_input: bfloat16 [160, 197, 768], P('dp')
- first_norm_gain_gradient: float32 [768], replicated
- grad_ln1_bias: float32 [768], replicated
- grad_w_qkv: float32 [3, 768, 768], P(None, None, 'tensor')
- grad_qv_bias: float32 [2, 768], P(None, 'tensor')
- grad_w_out: float32 [768, 768], P('tensor')
- grad_b_out: float32 [768], replicated
- second_norm_gain_gradient: float32 [768], replicated
- grad_ln2_bias: float32 [768], replicated
- grad_w_fc1: float32 [768, 3072], P(None, 'tensor')
- grad_b_fc1: float32 [3072], P('tensor')
- grad_w_fc2: float32 [3072, 768], P('tensor')
- grad_b_fc2: float32 [768], replicated
The draws below stay inside these ranges and needn't reach their ends.
All inputs are finite; a program needn't handle non-finite values. No bound on the sum of `image_counts` on one device may be relied on, other than what follows from the above.
Results may differ from the reference program's by a relative error of at most 0.012.
The reference program's roundings to bfloat16 on the way count: a program that leaves them out, or rounds other values in their place, can miss the bound.
Values sent between devices are 32-bit elements; how exact they have to be, the bound alone decides.
No kernel may reach another device: no remote copies, remote signals or barrier semaphores. Data moves between devices by JAX's collectives and lax.ppermute only.
A program may use at most 256 MiB of HBM per device.

```python
import math
import jax
import jax.numpy as jnp
import numpy as np
from jax import lax

D = 768
HD = 64
FF = 3072
S = 197
IMG_CAP = 10
IMAGES = 160
TOTAL_IMG = 88
N_DP = 16


def draw_w_qkv(key, part):
    base = jnp.clip(jax.random.normal(key, (3, D, D), jnp.float32), -6.0, 6.0) * D ** (-0.5)
    return base.astype(jnp.bfloat16)


def steps_of(rng, extent, split, low, largest):
    factor_of, own = 1.0, jax.random.fold_in(rng, 6)
    for dim, shards_of in split:
        steps = jnp.exp(jax.random.uniform(jax.random.fold_in(own, dim), (shards_of,), jnp.float32, low / len(split), largest / len(split)))
        factor_of = factor_of * jnp.repeat(steps, extent[dim] // shards_of).reshape([-1 if axis == dim else 1 for axis in range(len(extent))])
    return factor_of


def profile(amount, total, reach, lean):
    portions = [(1 << 20) // math.isqrt(grade ** lean) + 1 for grade in range(2, amount + 1)]
    surplus, counts = total - reach - (amount - 1), [1] * (amount - 1)
    while surplus > 0:
        movable = [i for i in range(amount - 1) if counts[i] < reach]
        whole, remaining = sum([portions[i] for i in movable]), surplus
        for i in movable:
            extra = min(reach - counts[i], max(1, remaining * portions[i] // whole), surplus)
            counts[i] = counts[i] + extra
            surplus = surplus - extra
    return np.array([reach] + counts)


def uneven_parts(stream_key, count, total, limit, skew):
    if count == 2:
        one = jax.random.randint(stream_key, (), max(1, total - limit), min(limit, total - 1) + 1)
        return jnp.stack([one, total - one])
    lengths = jnp.asarray(profile(count, total, limit, skew), jnp.int32)
    pairs = (count - 1) // 2
    source_of, taker = lengths[1:1 + 2 * pairs:2], lengths[2:2 + 2 * pairs:2]
    margin = jnp.minimum(source_of - 1, limit - taker)
    passed = jax.random.randint(jax.random.fold_in(stream_key, 1), (pairs,), 0, 1 << 20) % (margin + 1)
    lengths = lengths.at[1:1 + 2 * pairs:2].set(source_of - passed).at[2:2 + 2 * pairs:2].set(taker + passed)
    return lengths[jax.random.permutation(jax.random.fold_in(stream_key, 2), count)]


def noise(key, shape, deviation, bound, shards=(), dtype=jnp.bfloat16):
    drawn = jax.random.normal(key, shape, jnp.float32) * deviation
    if len(shards) > 0:
        drawn = steps_of(key, shape, shards, -0.22, 0.18) * drawn
    return jnp.clip(drawn, min=-bound, max=bound).astype(dtype)


def setup_inputs(seed: int = 0) -> dict:
    key_list = jax.random.split(jax.random.key(seed), 16)
    block_input = noise(key_list[0], (IMAGES, S, D), 1.0, 6.0, ((0, 16),))
    image_counts = uneven_parts(key_list[1], N_DP, TOTAL_IMG, IMG_CAP, 1).astype(jnp.int32)
    first_norm_gain = jnp.clip(1.0 + 0.18 * jax.random.normal(key_list[2], (D,), jnp.float32), 0.1, 1.9)
    first_norm_bias = noise(key_list[3], (D,), 0.5, 3.0, (), jnp.float32)
    w_qkv = draw_w_qkv(jax.random.fold_in(key_list[15], 71), 0)
    qv_bias = noise(key_list[5], (2, D), 0.5, 3.0, ((1, 2),), jnp.float32)
    w_out = noise(key_list[6], (D, D), HD ** -0.5, 0.75, ((0, 2),))
    b_out = noise(key_list[7], (D,), 0.5, 3.0, (), jnp.float32)
    second_norm_gain = jnp.clip(1.0 + 0.18 * jax.random.normal(key_list[8], (D,), jnp.float32), 0.1, 1.9)
    second_norm_bias = noise(key_list[9], (D,), 0.5, 3.0, (), jnp.float32)
    w_fc1 = noise(key_list[10], (D, FF), D ** -0.5, 0.21875, ((1, 2),))
    b_fc1 = noise(key_list[11], (FF,), 0.5, 3.0, ((0, 2),), jnp.float32)
    w_fc2 = noise(key_list[12], (FF, D), FF ** -0.5, 0.109375, ((0, 2),))
    b_fc2 = noise(key_list[13], (D,), 0.5, 3.0, (), jnp.float32)
    cotangent = noise(key_list[14], (IMAGES, S, D), 1.0, 6.0, ((0, 16),))
    return {"block_input": block_input, "image_counts": image_counts, "first_norm_gain": first_norm_gain, "first_norm_bias": first_norm_bias, "w_qkv": w_qkv, "qv_bias": qv_bias, "w_out": w_out, "b_out": b_out, "second_norm_gain": second_norm_gain, "second_norm_bias": second_norm_bias, "w_fc1": w_fc1, "b_fc1": b_fc1, "w_fc2": w_fc2, "b_fc2": b_fc2, "cotangent": cotangent}


EPSILON = 1e-06
INV_ROOT2 = 0.7071067811865476
INV_ROOT2PI = 0.3989422804014327

def apply_layer_norm(values, norm_gain, norm_bias):
    center = lax.optimization_barrier(jnp.mean(values, -1, keepdims=True))
    shifted = values - center
    spread = lax.optimization_barrier(jnp.mean(shifted * shifted, -1, keepdims=True))
    inv_std = lax.rsqrt(spread + EPSILON)
    normed = shifted * inv_std
    return (normed * norm_gain + norm_bias, normed, inv_std)

def norm_backward_pass(grad_normed, normed, inv_std, norm_gain):
    scaled = grad_normed * norm_gain
    first = lax.optimization_barrier(jnp.mean(scaled, -1, keepdims=True))
    second = lax.optimization_barrier(jnp.mean(scaled * normed, -1, keepdims=True))
    return inv_std * (scaled - first - normed * second)

def gelu_value(pre_act):
    return 0.5 * pre_act * (1.0 + lax.erf(pre_act * INV_ROOT2))

def gelu_slope(pre_act):
    return 0.5 * (1.0 + lax.erf(pre_act * INV_ROOT2)) + pre_act * jnp.exp(-0.5 * pre_act * pre_act) * INV_ROOT2PI

def shard_pass(block, live_count, cot_block, params):
    first_norm_gain, first_norm_bias, w_qkv, qv_bias, w_out, b_out, second_norm_gain, second_norm_bias, w_fc1, b_fc1, w_fc2, b_fc2 = params
    float_thirtytwo = jnp.float32
    bfloat_sixteen = jnp.bfloat16
    image_batch, sequence_length, model_width = block.shape
    total_rows = image_batch * sequence_length
    heads = w_qkv.shape[2] // HD
    local_width = heads * HD
    scale = HD ** (-0.5)
    live_rows = (jnp.arange(total_rows).astype(jnp.int32) // sequence_length < live_count)[:, None]
    input_tokens = block.reshape(total_rows, model_width).astype(float_thirtytwo)
    first_normed_tokens, first_centered_scaled, first_inverse_deviation = apply_layer_norm(input_tokens, first_norm_gain, first_norm_bias)
    normed_one_b = first_normed_tokens.astype(bfloat_sixteen)
    projected = jnp.einsum('nd,cde->cne', normed_one_b.astype(float_thirtytwo), w_qkv.astype(float_thirtytwo))
    shape4 = (image_batch, sequence_length, heads, HD)
    queries = (projected[0] + qv_bias[0]).astype(bfloat_sixteen).reshape(shape4)
    keys_all = projected[1].astype(bfloat_sixteen).reshape(shape4)
    values_all = (projected[2] + qv_bias[1]).astype(bfloat_sixteen).reshape(shape4)
    scores = jnp.einsum('ishd,ithd->ihst', queries.astype(float_thirtytwo), keys_all.astype(float_thirtytwo)) * scale
    log_total = jax.nn.logsumexp(scores, axis=-1)
    probs = jnp.exp(scores - log_total[..., None]).astype(bfloat_sixteen)
    context = jnp.einsum('ihst,ithd->ishd', probs.astype(float_thirtytwo), values_all.astype(float_thirtytwo)).astype(bfloat_sixteen).reshape(total_rows, local_width)
    attn_full = jnp.dot(context, w_out, preferred_element_type=float_thirtytwo)
    residual_stream = input_tokens + (attn_full + b_out)
    second_normed_tokens, second_centered_scaled, second_inverse_deviation = apply_layer_norm(residual_stream, second_norm_gain, second_norm_bias)
    normed_two_b = second_normed_tokens.astype(bfloat_sixteen)
    pre_act = jnp.dot(normed_two_b, w_fc1, preferred_element_type=float_thirtytwo) + b_fc1
    activated = gelu_value(pre_act).astype(bfloat_sixteen)
    mlp_full = jnp.dot(activated, w_fc2, preferred_element_type=float_thirtytwo)
    outputs = residual_stream + (mlp_full + b_fc2)
    block_out = jnp.where(live_rows, outputs, 0.0).astype(bfloat_sixteen).reshape(image_batch, sequence_length, model_width)
    output_gradient = jnp.where(live_rows, cot_block.reshape(total_rows, model_width), jnp.zeros((), bfloat_sixteen))
    grad_w_fc2 = jnp.dot(activated.T, output_gradient, preferred_element_type=float_thirtytwo)
    grad_b_fc2 = lax.optimization_barrier(jnp.sum(output_gradient.astype(float_thirtytwo), axis=0))
    grad_pre = (jnp.dot(output_gradient, w_fc2.T, preferred_element_type=float_thirtytwo) * gelu_slope(pre_act)).astype(bfloat_sixteen)
    grad_w_fc1 = jnp.dot(normed_two_b.T, grad_pre, preferred_element_type=float_thirtytwo)
    grad_b_fc1 = lax.optimization_barrier(jnp.sum(grad_pre.astype(float_thirtytwo), axis=0))
    second_normed_gradient = jnp.dot(grad_pre, w_fc1.T, preferred_element_type=float_thirtytwo)
    second_norm_gain_gradient = lax.optimization_barrier(jnp.sum(second_normed_gradient * second_centered_scaled, axis=0))
    grad_ln2_bias = lax.optimization_barrier(jnp.sum(second_normed_gradient, axis=0))
    residual_gradient = output_gradient.astype(float_thirtytwo) + norm_backward_pass(second_normed_gradient, second_centered_scaled, second_inverse_deviation, second_norm_gain)
    grad_resid_b = residual_gradient.astype(bfloat_sixteen)
    grad_w_out = jnp.dot(context.T, grad_resid_b, preferred_element_type=float_thirtytwo)
    grad_b_out = lax.optimization_barrier(jnp.sum(residual_gradient, axis=0))
    grad_context = jnp.dot(grad_resid_b, w_out.T, preferred_element_type=float_thirtytwo).astype(bfloat_sixteen).reshape(shape4)
    again = jnp.einsum('ishd,ithd->ihst', queries.astype(float_thirtytwo), keys_all.astype(float_thirtytwo)) * scale
    probs_full = jnp.exp(again - log_total[..., None])
    probs_again = probs_full.astype(bfloat_sixteen)
    grad_values = jnp.einsum('ihst,ishd->ithd', probs_again.astype(float_thirtytwo), grad_context.astype(float_thirtytwo)).astype(bfloat_sixteen)
    grad_probs = jnp.einsum('ishd,ithd->ihst', grad_context.astype(float_thirtytwo), values_all.astype(float_thirtytwo))
    row_dot = lax.optimization_barrier(jnp.sum(probs_full * grad_probs, axis=-1, keepdims=True))
    grad_scores = (probs_full * (grad_probs - row_dot)).astype(bfloat_sixteen)
    grad_queries = (jnp.einsum('ihst,ithd->ishd', grad_scores.astype(float_thirtytwo), keys_all.astype(float_thirtytwo)) * scale).astype(bfloat_sixteen)
    grad_keys = (jnp.einsum('ihst,ishd->ithd', grad_scores.astype(float_thirtytwo), queries.astype(float_thirtytwo)) * scale).astype(bfloat_sixteen)
    grad_proj = jnp.stack([grad_queries, grad_keys, grad_values]).reshape(3, total_rows, local_width)
    grad_w_qkv = jnp.einsum('nd,cne->cde', normed_one_b.astype(float_thirtytwo), grad_proj.astype(float_thirtytwo))
    grad_qv_bias = jnp.stack([lax.optimization_barrier(jnp.sum(grad_proj[0].astype(float_thirtytwo), axis=0)), lax.optimization_barrier(jnp.sum(grad_proj[2].astype(float_thirtytwo), axis=0))])
    first_normed_gradient = jnp.einsum('cne,cde->nd', grad_proj.astype(float_thirtytwo), w_qkv.astype(float_thirtytwo))
    first_norm_gain_gradient = lax.optimization_barrier(jnp.sum(first_normed_gradient * first_centered_scaled, axis=0))
    grad_ln1_bias = lax.optimization_barrier(jnp.sum(first_normed_gradient, axis=0))
    gradient_of_input = (residual_gradient + norm_backward_pass(first_normed_gradient, first_centered_scaled, first_inverse_deviation, first_norm_gain)).astype(bfloat_sixteen).reshape(image_batch, sequence_length, model_width)
    grads = (first_norm_gain_gradient, grad_ln1_bias, grad_w_qkv, grad_qv_bias, grad_w_out, grad_b_out, second_norm_gain_gradient, grad_ln2_bias, grad_w_fc1, grad_b_fc1, grad_w_fc2, grad_b_fc2)
    return (block_out, gradient_of_input, grads)

def reference(block_input, image_counts, first_norm_gain, first_norm_bias, w_qkv, qv_bias, w_out, b_out, second_norm_gain, second_norm_bias, w_fc1, b_fc1, w_fc2, b_fc2, cotangent):
    params = (first_norm_gain, first_norm_bias, w_qkv, qv_bias, w_out, b_out, second_norm_gain, second_norm_bias, w_fc1, b_fc1, w_fc2, b_fc2)
    blocks = block_input.reshape(N_DP, IMG_CAP, S, D)
    cot_blocks = cotangent.reshape(N_DP, IMG_CAP, S, D)
    start = tuple((jnp.zeros(param.shape, jnp.float32) for param in params))

    def step(carry, input_tokens):
        block, live_count, cot_block = input_tokens
        block_out, gradient_of_input, grads = shard_pass(block, live_count, cot_block, params)
        summed = tuple((total + piece for total, piece in zip(carry, grads)))
        return (summed, (block_out, gradient_of_input))
    totals, (outs, in_grads) = lax.scan(step, start, (blocks, image_counts.astype(jnp.int32), cot_blocks))
    block_out = outs.reshape(IMAGES, S, D)
    gradient_of_input = in_grads.reshape(IMAGES, S, D)
    return (block_out, gradient_of_input, totals[0], totals[1], totals[2], totals[3], totals[4], totals[5], totals[6], totals[7], totals[8], totals[9], totals[10], totals[11])
```

```python
import functools

import jax
import jax.numpy as jnp
from jax import lax
from jax.experimental import pallas as pl
from jax.experimental.pallas import tpu as pltpu
from jax.sharding import PartitionSpec as P

HD = 64
EPSILON = 1e-06
INV_ROOT2 = 0.7071067811865476
INV_ROOT2PI = 0.3989422804014327
F32 = jnp.float32
BF16 = jnp.bfloat16
IB = 2
LANES = 128
TILE = 256
VMEM_LIMIT = 60 * 1024 * 1024


def _nn(a, b):
    return lax.dot_general(a, b, (((1,), (0,)), ((), ())), preferred_element_type=F32)


def _nt(a, b):
    return lax.dot_general(a, b, (((1,), (1,)), ((), ())), preferred_element_type=F32)


def _tn(a, b):
    return lax.dot_general(a, b, (((0,), (0,)), ((), ())), preferred_element_type=F32)


def norm_stats(values):
    center = jnp.mean(values, -1, keepdims=True)
    shifted = values - center
    spread = jnp.mean(shifted * shifted, -1, keepdims=True)
    inv_std = lax.rsqrt(spread + EPSILON)
    return shifted * inv_std, inv_std


def norm_backward(grad_normed, normed, inv_std, gain):
    scaled = grad_normed * gain
    first = jnp.mean(scaled, -1, keepdims=True)
    second = jnp.mean(scaled * normed, -1, keepdims=True)
    return inv_std * (scaled - first - normed * second)


def row_sum(values):
    return jnp.sum(values, axis=0, keepdims=True)


def stack_heads(two):
    lane = lax.broadcasted_iota(jnp.int32, two.shape, 1)
    zero = jnp.zeros_like(two)
    return jnp.concatenate([jnp.where(lane < HD, two, zero), jnp.where(lane < HD, zero, two)], 0)


def merge_heads(stacked):
    rows = stacked.shape[0] // 2
    lane = lax.broadcasted_iota(jnp.int32, (rows, LANES), 1)
    return jnp.where(lane < HD, stacked[:rows], stacked[rows:])


def pair_probs(queries, keys, seq):
    scores = _nt(queries, keys) * (HD**-0.5)
    column = lax.broadcasted_iota(jnp.int32, scores.shape, 1)
    scores = jnp.where(column < seq, scores, jnp.finfo(F32).min)
    top = jnp.max(scores, -1, keepdims=True)
    weights = jnp.exp(scores - top)
    return weights * (1.0 / jnp.sum(weights, -1, keepdims=True))


def attention(qkv_ref, ctx_ref, seq):
    width = ctx_ref.shape[-1]
    for i in range(IB):
        for pair in range(width // LANES):
            at = [pl.ds(part * width + pair * LANES, LANES) for part in range(3)]
            probs = pair_probs(stack_heads(qkv_ref[i, :, at[0]]), qkv_ref[i, :, at[1]], seq)
            context = _nn(probs.astype(BF16), qkv_ref[i, :, at[2]])
            ctx_ref[i, :, pl.ds(pair * LANES, LANES)] = merge_heads(context).astype(BF16)


def project(normed, wcat_ref, qv_ref, qkv_ref):
    width = wcat_ref.shape[1] // 3
    rows = qkv_ref.shape[1]
    out = _nn(normed, wcat_ref[...])
    for part in range(3):
        piece = out[:, part * width : (part + 1) * width]
        if part != 1:
            piece = piece + qv_ref[part // 2 : part // 2 + 1, :]
        qkv_ref[:, :, pl.ds(part * width, width)] = piece.astype(BF16).reshape(IB, rows, width)


def load_images(x_ref, xs_ref):
    seq, rows = x_ref.shape[1], xs_ref.shape[0] // IB
    for i in range(IB):
        xs_ref[i * rows : i * rows + seq, :] = x_ref[i]
    return xs_ref[...].astype(F32)


def first_kernel(
    scal, x, cot, g1, b1, w_qkv, qv, w_out, n1_o, qkv_o, ctx_o, part_o, g_o, xs, wcat
):
    step = pl.program_id(0)
    width = w_out.shape[0]
    rows, model = n1_o.shape[1:]
    seq = x.shape[1]

    @pl.when(step == 0)
    def _():
        xs[...] = jnp.zeros_like(xs)
        for part in range(3):
            wcat[:, part * width : (part + 1) * width] = w_qkv[part]

    xhat, _ = norm_stats(load_images(x, xs))
    normed = (xhat * g1[...] + b1[...]).astype(BF16)
    n1_o[...] = normed.reshape(IB, rows, model)
    project(normed, wcat, qv, qkv_o)
    attention(qkv_o, ctx_o, seq)
    part_o[...] = _nn(ctx_o[...].reshape(IB * rows, width), w_out[...]).reshape(part_o.shape)
    g_o[...] = jnp.zeros_like(g_o)
    for i in range(IB):
        live = step * IB + i < scal[0]
        g_o[i, 0:seq, :] = jnp.where(live, cot[i], jnp.zeros_like(cot[i]))


def second_kernel(pieces, scal, n1, x, part, qv, b_out, g2, b2, *refs):
    wq_p, wo_p = refs[:pieces], refs[pieces : 2 * pieces]
    qkv_o, ctx_o, wcat, wout, resid_o, n2_o, xs = refs[2 * pieces :]
    step = pl.program_id(0)
    width = wout.shape[0]
    rows, model = n1.shape[1:]
    seq = x.shape[1]

    @pl.when(step == 0)
    def _():
        xs[...] = jnp.zeros_like(xs)
        for p in range(pieces):
            at = p ^ scal[1]
            high = wq_p[p].shape[1]
            where = pl.ds(pl.multiple_of(at * high, 16), high)
            for part in range(3):
                wcat[where, part * width : (part + 1) * width] = wq_p[p][part].astype(BF16)
            high = wo_p[p].shape[0]
            wout[pl.ds(pl.multiple_of(at * high, 16), high), :] = wo_p[p][...].astype(BF16)

    project(n1[...].reshape(IB * rows, model), wcat, qv, qkv_o)
    attention(qkv_o, ctx_o, seq)
    full = part[...].reshape(IB * rows, model) + _nn(
        ctx_o[...].reshape(IB * rows, width), wout[...]
    )
    resid = load_images(x, xs) + (full + b_out[...])
    resid_o[...] = resid.reshape(resid_o.shape)
    xhat, _ = norm_stats(resid)
    n2_o[...] = (xhat * g2[...] + b2[...]).astype(BF16).reshape(n2_o.shape)


def gelu_and_slope(pre):
    bell = 0.5 * (1.0 + lax.erf(pre * INV_ROOT2))
    return pre * bell, bell + pre * jnp.exp(-0.5 * pre * pre) * INV_ROOT2PI


def split_blocks(me, full, send, keep):
    half, high = keep.shape[:2]
    for p in range(half):
        for ref, at in ((keep, p), (send, p + half)):
            ref[p] = full[pl.ds(pl.multiple_of((at ^ me) * high, 8), high), :]


def mlp_a_kernel(scal, n2, fc1, bfc1, g_all, act_o, slope_o, send, keep, act_all, full):
    step = pl.program_id(0)
    rows, model = n2.shape[1:]
    tokens = n2[...].reshape(IB * rows, model)
    here = pl.ds(pl.multiple_of(step * IB * rows, 16), IB * rows)
    for j in range(fc1.shape[1] // TILE):
        cols = pl.ds(j * TILE, TILE)
        act, slope = gelu_and_slope(_nn(tokens, fc1[:, cols]) + bfc1[:, cols])
        act = act.astype(BF16)
        act_all[here, cols] = act
        act_o[:, :, cols] = act.reshape(IB, rows, TILE)
        slope_o[:, :, cols] = slope.reshape(IB, rows, TILE)

    @pl.when(step == pl.num_programs(0) - 1)
    def _():
        strip = 384
        for r in range(full.shape[0] // strip):
            cols = pl.ds(r * strip, strip)
            full[cols, :] = _tn(act_all[:, cols], g_all[...])
        split_blocks(scal[2], full, send, keep)


def mlp_b_kernel(
    scal, act, slope, g, n2_all, fc1, fc2, mlp_o, gn2_o, send, keep, gb_o, gpre_all, full
):
    step = pl.program_id(0)
    rows, model = g.shape[1:]
    hidden = fc1.shape[1]
    here = pl.ds(pl.multiple_of(step * IB * rows, 16), IB * rows)

    @pl.when(step == 0)
    def _():
        gb_o[...] = jnp.zeros_like(gb_o)

    grad_out = g[...].reshape(IB * rows, model)
    for j in range(hidden // TILE):
        cols = pl.ds(j * TILE, TILE)
        grad = _nt(grad_out, fc2[cols, :]) * slope[:, :, cols].reshape(IB * rows, TILE)
        grad = grad.astype(BF16)
        gpre_all[here, cols] = grad
        gb_o[:, cols] += row_sum(grad.astype(F32))
    mlp_o[...] = _nn(act[...].reshape(IB * rows, hidden), fc2[...]).reshape(mlp_o.shape)
    gn2_o[...] = _nt(gpre_all[here, :], fc1[...]).reshape(gn2_o.shape)

    @pl.when(step == pl.num_programs(0) - 1)
    def _():
        strip = 384
        for r in range(full.shape[0] // strip):
            cols = pl.ds(r * strip, strip)
            full[cols, :] = _tn(n2_all[:, cols], gpre_all[...])
        split_blocks(scal[3], full, send, keep)


def mlp_c_kernel(pieces, scal, n2, g, resid, mlp_p, gn2_p, bfc1, g2, bfc2, *refs):
    fc1_p, fc2_p = refs[:pieces], refs[pieces : 2 * pieces]
    out_o, gr_o, grb_o, sums, fc1, fc2, gpre, act_s = refs[2 * pieces :]
    step = pl.program_id(0)
    rows, model = n2.shape[1:]
    hidden = fc1.shape[1]
    seq = out_o.shape[1]

    @pl.when(step == 0)
    def _():
        sums[...] = jnp.zeros_like(sums)
        for p in range(pieces):
            at = p ^ scal[4]
            for source, target in ((fc1_p[p], fc1), (fc2_p[p], fc2)):
                high = source.shape[0]
                target[pl.ds(pl.multiple_of(at * high, 16), high), :] = source[...].astype(BF16)

    tokens = n2[...].reshape(IB * rows, model)
    grad_out = g[...].reshape(IB * rows, model)
    for j in range(hidden // TILE):
        cols = pl.ds(j * TILE, TILE)
        act, slope = gelu_and_slope(_nn(tokens, fc1[:, cols]) + bfc1[:, cols])
        act_s[:, cols] = act.astype(BF16)
        gpre[:, cols] = (_nt(grad_out, fc2[cols, :]) * slope).astype(BF16)
    mlp_full = mlp_p[...].reshape(IB * rows, model) + _nn(act_s[...], fc2[...])
    gn2 = gn2_p[...].reshape(IB * rows, model) + _nt(gpre[...], fc1[...])
    residual = resid[...].reshape(IB * rows, model)
    out = residual + (mlp_full + bfc2[...])
    for i in range(IB):
        live = step * IB + i < scal[0]
        out_o[i] = jnp.where(live, out[i * rows : i * rows + seq], 0.0).astype(BF16)
    xhat, inv = norm_stats(residual)
    grad_f = grad_out.astype(F32)
    grad_resid = grad_f + norm_backward(gn2, xhat, inv, g2[...])
    sums[0:1] += row_sum(gn2 * xhat)
    sums[1:2] += row_sum(gn2)
    sums[2:3] += row_sum(grad_resid)
    sums[3:4] += row_sum(grad_f)
    gr_o[...] = grad_resid.reshape(gr_o.shape)
    grb_o[...] = grad_resid.astype(BF16).reshape(grb_o.shape)


def attention_backward(qkv_ref, gctx, dq_ref, start, seq):
    width = gctx.shape[1]
    rows = qkv_ref.shape[1]
    scale = HD**-0.5
    for i in range(IB):
        where = pl.ds(pl.multiple_of(start + i * rows, 16), rows)
        for pair in range(width // LANES):
            at = [pl.ds(part * width + pair * LANES, LANES) for part in range(3)]
            queries = stack_heads(qkv_ref[i, :, at[0]])
            keys, values = qkv_ref[i, :, at[1]], qkv_ref[i, :, at[2]]
            probs = pair_probs(queries, keys, seq)
            grad = stack_heads(
                gctx[i * rows : (i + 1) * rows, pair * LANES : (pair + 1) * LANES]
            )
            grad_probs = _nt(grad, values)
            dot = jnp.sum(probs * grad_probs, -1, keepdims=True)
            grad_scores = (probs * (grad_probs - dot)).astype(BF16)
            dq_ref[where, at[2]] = _tn(probs.astype(BF16), grad).astype(BF16)
            dq_ref[where, at[0]] = merge_heads(_nn(grad_scores, keys) * scale).astype(BF16)
            dq_ref[where, at[1]] = (_tn(grad_scores, queries) * scale).astype(BF16)


def own_backward_kernel(
    seq,
    scal,
    grb,
    qkv,
    w_qkv,
    w_out,
    n1_all,
    ctx_all,
    grb_all,
    gn1_o,
    send,
    keep,
    gqv_o,
    dq_all,
    wcat,
    full_q,
    full_o,
):
    step = pl.program_id(0)
    rows, model = grb.shape[1:]
    width = w_out.shape[0]

    @pl.when(step == 0)
    def _():
        gqv_o[...] = jnp.zeros_like(gqv_o)
        for part in range(3):
            wcat[:, part * width : (part + 1) * width] = w_qkv[part]

    start = step * IB * rows
    here = pl.ds(pl.multiple_of(start, 16), IB * rows)
    gctx = _nt(grb[...].reshape(IB * rows, model), w_out[...]).astype(BF16)
    attention_backward(qkv, gctx, dq_all, start, seq)
    gn1_o[...] = _nt(dq_all[here, :], wcat[...]).reshape(gn1_o.shape)
    gqv_o[0:1] += row_sum(dq_all[here, 0:width].astype(F32))
    gqv_o[1:2] += row_sum(dq_all[here, 2 * width : 3 * width].astype(F32))

    @pl.when(step == pl.num_programs(0) - 1)
    def _():
        for part in range(3):
            cols = pl.ds(part * width, width)
            full_q[pl.ds(part * model, model), :] = _tn(n1_all[...], dq_all[:, cols])
        full_o[...] = _tn(ctx_all[...], grb_all[...])
        half = keep.shape[0]
        high_q, high_o = full_q.shape[0] // (2 * half), width // (2 * half)
        for p in range(half):
            for ref, at in ((keep, p), (send, p + half)):
                block = at ^ scal[5]
                from_q = pl.ds(pl.multiple_of(block * high_q, 8), high_q)
                from_o = pl.ds(pl.multiple_of(block * high_o, 8), high_o)
                ref[p, 0:high_q, :] = full_q[from_q, :]
                for c in range(model // width):
                    ref[p, high_q + c * high_o : high_q + (c + 1) * high_o, :] = full_o[
                        from_o, c * width : (c + 1) * width
                    ]


def other_backward_kernel(
    scal, grb, qkv, wcat, w_out, gn1_p, gr, x, g1, gin_o, sums, dq, xs
):
    step = pl.program_id(0)
    rows, model = grb.shape[1:]
    seq = x.shape[1]

    @pl.when(step == 0)
    def _():
        sums[...] = jnp.zeros_like(sums)
        xs[...] = jnp.zeros_like(xs)

    gctx = _nt(grb[...].reshape(IB * rows, model), w_out[...]).astype(BF16)
    attention_backward(qkv, gctx, dq, 0, seq)
    gn1 = gn1_p[...].reshape(IB * rows, model) + _nt(dq[...], wcat[...])
    xhat, inv = norm_stats(load_images(x, xs))
    sums[0:1] += row_sum(gn1 * xhat)
    sums[1:2] += row_sum(gn1)
    grad = gr[...].reshape(IB * rows, model) + norm_backward(gn1, xhat, inv, g1[...])
    for i in range(IB):
        gin_o[i] = grad[i * rows : i * rows + seq].astype(BF16)


def portion_kernel(count, scal, *refs):
    for source, target in zip(refs[:count], refs[count:]):
        axis = len(source.shape) - 2
        high = target.shape[axis]
        where = pl.ds(pl.multiple_of(scal[0] * high, 16), high)
        if axis:
            target[...] = source[:, where, :].astype(F32)
        else:
            target[...] = source[where, :].astype(F32)


def _whole(shape):
    return pl.BlockSpec(shape, lambda i, *_: (0,) * len(shape), pipeline_mode=pl.Buffered(1))


def _images(*tail):
    return pl.BlockSpec((IB,) + tail, lambda i, *_: (i,) + (0,) * len(tail))


def _acc(shape):
    return pl.BlockSpec(shape, lambda i, *_: (0,) * len(shape))


def _call(kernel, name, grid, scalars, ins, outs, scratch, flops):
    moved = sum(a.size * a.dtype.itemsize for a, _ in ins)
    return pl.pallas_call(
        kernel,
        name=name,
        grid_spec=pltpu.PrefetchScalarGridSpec(
            num_scalar_prefetch=1,
            grid=(grid,),
            in_specs=[spec for _, spec in ins],
            out_specs=[spec for _, _, spec in outs],
            scratch_shapes=scratch,
        ),
        out_shape=[jax.ShapeDtypeStruct(shape, dtype) for shape, dtype, _ in outs],
        compiler_params=pltpu.CompilerParams(
            dimension_semantics=("arbitrary",), vmem_limit_bytes=VMEM_LIMIT
        ),
        cost_estimate=pl.CostEstimate(
            flops=int(flops), bytes_accessed=int(2 * moved), transcendentals=0
        ),
    )(scalars, *[a for a, _ in ins])


class Exchange:
    def __init__(self, size):
        self.size = size
        self.bits = size.bit_length() - 1

    def swap(self, value, bit):
        pairs = [(i, i ^ (1 << bit)) for i in range(self.size)]
        return lax.ppermute(value, "dp", pairs)

    def relative(self, index, order):
        out = jnp.int32(0)
        for bit in order:
            out = out * 2 + ((index >> bit) & 1)
        return out

    def reduce(self, send, keep, order):
        for n, bit in enumerate(order):
            got = self.swap(send, bit)
            half = keep.shape[0] // 2
            if n + 1 < len(order):
                send, keep = keep[half:] + got[half:], keep[:half] + got[:half]
            else:
                keep = keep + got
        for bit in range(self.bits):
            if bit not in order:
                keep = keep + self.swap(keep, bit)
        return keep

    def gather(self, block, order):
        for bit in reversed(order):
            block = jnp.concatenate([block, self.swap(block, bit)], 0)
        return block


def restore(me, blocks, unpack=None):
    n, high, wide = blocks.shape

    def kernel(scal, source, *targets):
        del scal
        if unpack is None:
            targets[0][...] = source[...]
        else:
            unpack(source, targets)

    if unpack is None:
        shapes = [(high, wide)]
    else:
        shapes = unpack.shapes
    return pl.pallas_call(
        kernel,
        name="restore",
        grid_spec=pltpu.PrefetchScalarGridSpec(
            num_scalar_prefetch=1,
            grid=(n,),
            in_specs=[pl.BlockSpec((None, high, wide), lambda p, me: (p, 0, 0))],
            out_specs=[pl.BlockSpec(s, lambda p, me: (p ^ me[0], 0)) for s in shapes],
        ),
        out_shape=[jax.ShapeDtypeStruct((n * s[0], s[1]), F32) for s in shapes],
    )(me.reshape(1), blocks)


class Unpack:
    def __init__(self, high_q, high_o, width, model):
        self.high_q, self.high_o, self.width = high_q, high_o, width
        self.shapes = [(high_q, width), (high_o, model)]

    def __call__(self, source, targets):
        targets[0][...] = source[0 : self.high_q, :]
        for c in range(self.shapes[1][1] // self.width):
            start = self.high_q + c * self.high_o
            targets[1][:, c * self.width : (c + 1) * self.width] = source[
                start : start + self.high_o, :
            ]


def shards(
    dp_size,
    block_input,
    image_counts,
    first_norm_gain,
    first_norm_bias,
    w_qkv,
    qv_bias,
    w_out,
    b_out,
    second_norm_gain,
    second_norm_bias,
    w_fc1,
    b_fc1,
    w_fc2,
    b_fc2,
    cotangent,
):
    images, seq, model = block_input.shape
    width = w_qkv.shape[2]
    hidden = w_fc1.shape[1]
    rows = -(-seq // 16) * 16
    steps = images // IB
    tokens = images * rows
    net = Exchange(dp_size)
    index = lax.axis_index("dp").astype(jnp.int32)
    order_a = order_b = order_c = (0, 1, 2, 3)
    near = (0,)
    pieces = 1 << len(near)
    blocks = 1 << len(order_a)
    half = blocks // 2
    me_near = net.relative(index, near[::-1])
    me_a, me_b, me_c = (net.relative(index, o) for o in (order_a, order_b, order_c))
    scal = jnp.stack(
        [image_counts[0].astype(jnp.int32), me_near, me_a, me_b, me_near, me_c]
    )
    row = lambda v: v.reshape(1, -1)

    def cross(value):
        return lax.ppermute(value, "tensor", [(0, 1), (1, 0)])

    def fetch(weights):
        shapes = []
        for w in weights:
            shape = list(w.shape)
            shape[-2] //= pieces
            shapes.append(tuple(shape))
        mine = pl.pallas_call(
            functools.partial(portion_kernel, len(weights)),
            name="portion",
            in_specs=[pl.BlockSpec(memory_space=pltpu.SMEM)]
            + [pl.BlockSpec(memory_space=pltpu.VMEM)] * len(weights),
            out_specs=[pl.BlockSpec(memory_space=pltpu.VMEM)] * len(weights),
            out_shape=[jax.ShapeDtypeStruct(s, F32) for s in shapes],
        )(me_near.reshape(1), *weights)
        held = [[cross(m)] for m in mine]
        for bit in near:
            held = [h + [net.swap(piece, bit) for piece in h] for h in held]
        return held

    wq_o, wo_o = fetch([w_qkv, w_out])
    fc1_o, fc2_o = fetch([w_fc1, w_fc2])
    qv_o, bfc1_o = cross(qv_bias), cross(b_fc1)

    flop = 2.0 * tokens * model
    n1, qkv, ctx, part, g = _call(
        first_kernel,
        "first",
        steps,
        scal,
        [
            (block_input, _images(seq, model)),
            (cotangent, _images(seq, model)),
            (row(first_norm_gain), _whole((1, model))),
            (row(first_norm_bias), _whole((1, model))),
            (w_qkv, _whole(w_qkv.shape)),
            (qv_bias, _whole(qv_bias.shape)),
            (w_out, _whole(w_out.shape)),
        ],
        [
            ((images, rows, model), BF16, _images(rows, model)),
            ((images, rows, 3 * width), BF16, _images(rows, 3 * width)),
            ((images, rows, width), BF16, _images(rows, width)),
            ((images, rows, model), F32, _images(rows, model)),
            ((images, rows, model), BF16, _images(rows, model)),
        ],
        [pltpu.VMEM((IB * rows, model), BF16), pltpu.VMEM((model, 3 * width), BF16)],
        flop * 5 * width,
    )
    qkv2, ctx2, wcat2, wout2, resid, n2 = _call(
        functools.partial(second_kernel, pieces),
        "second",
        steps,
        scal,
        [
            (n1, _images(rows, model)),
            (block_input, _images(seq, model)),
            (part, _images(rows, model)),
            (qv_o, _whole(qv_o.shape)),
            (row(b_out), _whole((1, model))),
            (row(second_norm_gain), _whole((1, model))),
            (row(second_norm_bias), _whole((1, model))),
        ]
        + [(w, _whole(w.shape)) for w in wq_o]
        + [(w, _whole(w.shape)) for w in wo_o],
        [
            ((images, rows, 3 * width), BF16, _images(rows, 3 * width)),
            ((images, rows, width), BF16, _images(rows, width)),
            ((model, 3 * width), BF16, _acc((model, 3 * width))),
            ((width, model), BF16, _acc((width, model))),
            ((images, rows, model), F32, _images(rows, model)),
            ((images, rows, model), BF16, _images(rows, model)),
        ],
        [pltpu.VMEM((IB * rows, model), BF16)],
        flop * 5 * width,
    )
    del ctx2
    act, slope, send_a, keep_a = _call(
        mlp_a_kernel,
        "mlp_a",
        steps,
        scal,
        [
            (n2, _images(rows, model)),
            (w_fc1, _whole(w_fc1.shape)),
            (row(b_fc1), _whole((1, hidden))),
            (g.reshape(tokens, model), _whole((tokens, model))),
        ],
        [
            ((images, rows, hidden), BF16, _images(rows, hidden)),
            ((images, rows, hidden), F32, _images(rows, hidden)),
            ((half, hidden // blocks, model), F32, _acc((half, hidden // blocks, model))),
            ((half, hidden // blocks, model), F32, _acc((half, hidden // blocks, model))),
        ],
        [pltpu.VMEM((tokens, hidden), BF16), pltpu.VMEM((hidden, model), F32)],
        flop * 2 * hidden,
    )
    mlp_p, gn2_p, send_b, keep_b, gb1 = _call(
        mlp_b_kernel,
        "mlp_b",
        steps,
        scal,
        [
            (act, _images(rows, hidden)),
            (slope, _images(rows, hidden)),
            (g, _images(rows, model)),
            (n2.reshape(tokens, model), _whole((tokens, model))),
            (w_fc1, _whole(w_fc1.shape)),
            (w_fc2, _whole(w_fc2.shape)),
        ],
        [
            ((images, rows, model), F32, _images(rows, model)),
            ((images, rows, model), F32, _images(rows, model)),
            ((half, model // blocks, hidden), F32, _acc((half, model // blocks, hidden))),
            ((half, model // blocks, hidden), F32, _acc((half, model // blocks, hidden))),
            ((1, hidden), F32, _acc((1, hidden))),
        ],
        [pltpu.VMEM((tokens, hidden), BF16), pltpu.VMEM((model, hidden), F32)],
        flop * 4 * hidden,
    )
    block_out, gr, grb, sums2 = _call(
        functools.partial(mlp_c_kernel, pieces),
        "mlp_c",
        steps,
        scal,
        [
            (n2, _images(rows, model)),
            (g, _images(rows, model)),
            (resid, _images(rows, model)),
            (mlp_p, _images(rows, model)),
            (gn2_p, _images(rows, model)),
            (row(bfc1_o), _whole((1, hidden))),
            (row(second_norm_gain), _whole((1, model))),
            (row(b_fc2), _whole((1, model))),
        ]
        + [(w, _whole(w.shape)) for w in fc1_o]
        + [(w, _whole(w.shape)) for w in fc2_o],
        [
            ((images, seq, model), BF16, _images(seq, model)),
            ((images, rows, model), F32, _images(rows, model)),
            ((images, rows, model), BF16, _images(rows, model)),
            ((8, model), F32, _acc((8, model))),
        ],
        [
            pltpu.VMEM((model, hidden), BF16),
            pltpu.VMEM((hidden, model), BF16),
            pltpu.VMEM((IB * rows, hidden), BF16),
            pltpu.VMEM((IB * rows, hidden), BF16),
        ],
        flop * 4 * hidden,
    )
    packed = (3 * model + model) // blocks
    gn1_p, send_c, keep_c, gqv = _call(
        functools.partial(own_backward_kernel, seq),
        "own_backward",
        steps,
        scal,
        [
            (grb, _images(rows, model)),
            (qkv, _images(rows, 3 * width)),
            (w_qkv, _whole(w_qkv.shape)),
            (w_out, _whole(w_out.shape)),
            (n1.reshape(tokens, model), _whole((tokens, model))),
            (ctx.reshape(tokens, width), _whole((tokens, width))),
            (grb.reshape(tokens, model), _whole((tokens, model))),
        ],
        [
            ((images, rows, model), F32, _images(rows, model)),
            ((half, packed, width), F32, _acc((half, packed, width))),
            ((half, packed, width), F32, _acc((half, packed, width))),
            ((2, width), F32, _acc((2, width))),
        ],
        [
            pltpu.VMEM((tokens, 3 * width), BF16),
            pltpu.VMEM((model, 3 * width), BF16),
            pltpu.VMEM((3 * model, width), F32),
            pltpu.VMEM((width, model), F32),
        ],
        flop * 10 * width,
    )
    gin, sums1 = _call(
        other_backward_kernel,
        "other_backward",
        steps,
        scal,
        [
            (grb, _images(rows, model)),
            (qkv2, _images(rows, 3 * width)),
            (wcat2, _whole(wcat2.shape)),
            (wout2, _whole(wout2.shape)),
            (gn1_p, _images(rows, model)),
            (gr, _images(rows, model)),
            (block_input, _images(seq, model)),
            (row(first_norm_gain), _whole((1, model))),
        ],
        [
            ((images, seq, model), BF16, _images(seq, model)),
            ((8, model), F32, _acc((8, model))),
        ],
        [
            pltpu.VMEM((IB * rows, 3 * width), BF16),
            pltpu.VMEM((IB * rows, model), BF16),
        ],
        flop * 6 * width,
    )

    def total(send, keep, order):
        return net.gather(net.reduce(send, keep, order), order)

    (grad_fc2,) = restore(me_a, total(send_a, keep_a, order_a))
    (grad_fc1,) = restore(me_b, total(send_b, keep_b, order_b))
    grad_qkv, grad_out = restore(
        me_c,
        total(send_c, keep_c, order_c),
        Unpack(3 * model // blocks, width // blocks, width, model),
    )
    small = jnp.concatenate(
        [sums1[0:2].ravel(), sums2[0:4].ravel(), gqv.ravel(), gb1.ravel()]
    )
    pad = -small.size % (8 * LANES)
    small = jnp.pad(small, (0, pad)).reshape(-1, LANES)
    for bit in range(net.bits):
        small = small + net.swap(small, bit)
    small = small.ravel()
    cut = lambda start, size: small[start : start + size]
    base = 6 * model
    return (
        block_out,
        gin,
        cut(0, model),
        cut(model, model),
        grad_qkv.reshape(3, model, width),
        cut(base, 2 * width).reshape(2, width),
        grad_out,
        cut(4 * model, model),
        cut(2 * model, model),
        cut(3 * model, model),
        grad_fc1,
        cut(base + 2 * width, hidden),
        grad_fc2,
        cut(5 * model, model),
    )


def solution(mesh):
    in_specs = (
        P("dp", None, None),
        P("dp"),
        P(),
        P(),
        P(None, None, "tensor"),
        P(None, "tensor"),
        P("tensor", None),
        P(),
        P(),
        P(),
        P(None, "tensor"),
        P("tensor"),
        P("tensor", None),
        P(),
        P("dp", None, None),
    )
    out_specs = (
        P("dp", None, None),
        P("dp", None, None),
        P(),
        P(),
        P(None, None, "tensor"),
        P(None, "tensor"),
        P("tensor", None),
        P(),
        P(),
        P(),
        P(None, "tensor"),
        P("tensor"),
        P("tensor", None),
        P(),
    )
    return jax.shard_map(
        functools.partial(shards, mesh.shape["dp"]),
        mesh=mesh,
        in_specs=in_specs,
        out_specs=out_specs,
        check_vma=False,
    )
```
